128 devices in a mesh: samples: 8 (over y, x_hi), space: 16 (over x_lo, z, core).
Axes of the slice: x: 4 (x_hi: 2, x_lo: 2; x = x_hi * 2 + x_lo), y: 4, z: 4, core: 2. Of those that a mesh axis runs over, the one named last changes fastest.
Arguments:
- target: bfloat16 [8, 16384, 8192], P(None, 'samples', 'space'), may hold values from 0 to 1
- a_factor: bfloat16 [16384, 256], P(('samples', 'space')), may hold values from -3 to 3
- b_factor: bfloat16 [8192, 256], P(('space', 'samples')), may hold values from -3 to 3
- c_factor: bfloat16 [8, 256], replicated, may hold values from -3 to 3
Outputs:
- grad_a: float32 [16384, 256], P(('samples', 'space'))
- grad_b: float32 [8192, 256], P(('space', 'samples'))
- grad_c: float32 [8, 256], replicated
The draws below stay inside these ranges and needn't reach their ends.
All inputs are finite; a program needn't handle non-finite values.
Results may differ from the reference program's by a relative error of at most 0.002.
Values may be sent and summed in bfloat16 or wider, within the bound.
No kernel may reach another device: no remote copies, remote signals or barrier semaphores. Data moves between devices by JAX's collectives and lax.ppermute only.
A program may use at most 128 MiB of HBM per device.

```python
import jax
import jax.numpy as jnp
from jax import lax

R = 256
K = 8
I = 16384
J = 8192


def block_scale(rng, dims, shards, low, top_value):
    level = 1.0
    for dim, shards_of in shards:
        steps = jax.random.uniform(jax.random.fold_in(jax.random.fold_in(rng, 6), dim), (shards_of,), jnp.float32, low / len(shards), top_value / len(shards))
        level = level * jnp.repeat(jnp.exp(steps), dims[dim] // shards_of).reshape((-1,) + (1,) * (len(dims) - 1 - dim))
    return level


def normal_values(rng, shape, scale, reach, pieces=(), kind=jnp.bfloat16):
    entries = scale * jax.random.normal(rng, shape, jnp.float32)
    if pieces:
        entries = entries * block_scale(rng, shape, pieces, -0.22, 0.18)
    return jnp.clip(entries, -reach, reach).astype(kind)


def setup_inputs(seed: int = 0) -> dict:
    streams_of = jax.random.split(jax.random.key(seed), 5)
    return {
        "target": jnp.clip(1.0 * jax.random.uniform(streams_of[0], (K, I, J), jnp.float32) ** block_scale(streams_of[0], (K, I, J), ((1, 8), (2, 16)), -0.2, 0.2), 0.0, 1.0).astype(jnp.bfloat16),
        "a_factor": normal_values(streams_of[1], (I, R), 0.5, 3.0, ((0, 128),)),
        "b_factor": normal_values(streams_of[2], (J, R), 0.5, 3.0, ((0, 128),)),
        "c_factor": normal_values(streams_of[3], (K, R), 0.5, 3.0),
    }


def reference(target, a_factor, b_factor, c_factor):
    b_wide = b_factor.astype(jnp.float32)
    a_wide = a_factor.astype(jnp.float32)

    def per_step(carry, inputs):
        grad_a, grad_b = carry
        slab, c_row = inputs
        c_wide = c_row.astype(jnp.float32)
        scaled = (a_wide * c_wide[None, :]).astype(jnp.bfloat16)
        model = jnp.dot(scaled, b_factor.T, preferred_element_type=jnp.float32)
        derivative = (jax.nn.sigmoid(model) - slab.astype(jnp.float32)).astype(jnp.bfloat16)
        inner = jnp.dot(derivative, b_factor, preferred_element_type=jnp.float32)
        weighted = jnp.dot(derivative.T, a_factor, preferred_element_type=jnp.float32)
        grad_a = grad_a + inner * c_wide[None, :]
        grad_b = grad_b + weighted * c_wide[None, :]
        grad_c_row = jnp.sum(weighted * b_wide, axis=0)
        return (grad_a, grad_b), grad_c_row

    start = (jnp.zeros(a_factor.shape, jnp.float32), jnp.zeros(b_factor.shape, jnp.float32))
    (grad_a, grad_b), grad_c = lax.scan(per_step, start, (target, c_factor))
    return grad_a, grad_b, grad_c
```

```python
import jax
import jax.numpy as jnp
from jax import lax
from jax.experimental import pallas as pl
from jax.experimental.pallas import tpu as pltpu
from jax.sharding import PartitionSpec as P

F32 = jnp.float32
BF16 = jnp.bfloat16
K, R = 8, 256
SHARD = 128
NJ = 512
XL, Z, CORE = 2, 4, 2

SPACE = range(XL * Z * CORE)
SAME_CORE = [[2 * g + c for g in range(XL * Z)] for c in range(CORE)]
TO_CORE = [(p, p ^ 1) for p in SPACE]
TO_XL = [(p, p ^ 8) for p in SPACE]


def from_z(d):
    return [((p & 9) | ((((p >> 1) + d) % 4) << 1), p) for p in SPACE]


def dot_last(x, y):
    return lax.dot_general(x, y, (((1,), (1,)), ((), ())), preferred_element_type=F32)


def dot(x, y):
    return jnp.dot(x, y, preferred_element_type=F32)


def body(table, t0, t1, t2, t3, a_ref, b_ref, ch_ref, cht_ref, bt_ref, same_ref, other_ref, gb_ref, gc_ref, w_ref):
    step = pl.program_id(0)
    rows = a_ref[0]
    wide = rows.astype(F32)
    rows_t = rows.T
    b = b_ref[...]
    grad = jnp.zeros((4 * SHARD, R), F32)
    for k in range(K):
        ck = ch_ref[k : k + 1, :]
        half = dot_last((wide * ck).astype(BF16), b)
        t = jnp.concatenate([r[k, 0] for r in (t0, t1, t2, t3)], axis=0).astype(F32)
        d2 = ((jnp.tanh(half) + 1.0) - (t + t)).astype(BF16)
        grad = grad + dot(d2, b) * ck
        part = dot(rows_t, d2)
        w_ref[k] = jnp.where(step > 0, w_ref[k], 0.0) + part

    xl = table[16]
    for dx in range(2):
        at = lax.bitwise_xor(xl, dx)
        same_ref[at, 0] = grad[dx * SHARD : (dx + 1) * SHARD]
        other_ref[at, 0] = grad[(2 + dx) * SHARD : (3 + dx) * SHARD]

    @pl.when(step == pl.num_programs(0) - 1)
    def _():
        total = jnp.zeros((R, NJ), F32)
        lane = lax.broadcasted_iota(jnp.int32, (R, 128), 1)
        sums = jnp.zeros((R, 128), F32)
        bt = bt_ref[...].astype(F32)
        for k in range(K):
            wk = w_ref[k]
            total = total + wk * cht_ref[:, k : k + 1]
            s = jnp.sum(wk * bt, axis=1, keepdims=True) * 0.5
            sums = jnp.where(lane == k, s, sums)
        gb_ref[...] = total.T
        gc_ref[...] = sums.T[:K]


def local(table, target, a_all, b_full, c_half):
    def tile(q):
        return pl.BlockSpec((K, 1, SHARD, NJ), lambda s, tab: (0, tab[s * 4 + q], 0, 0))

    def whole(*shape):
        return pl.BlockSpec(shape, lambda s, tab: (0,) * len(shape))

    out = pl.BlockSpec((XL, 1, SHARD, R), lambda s, tab: (0, tab[17 + s], 0, 0))
    return pl.pallas_call(
        body,
        grid_spec=pltpu.PrefetchScalarGridSpec(
            num_scalar_prefetch=1,
            grid=(Z,),
            in_specs=[tile(0), tile(1), tile(2), tile(3),
                      pl.BlockSpec((1, 4 * SHARD, R), lambda s, tab: (s, 0, 0)),
                      whole(NJ, R), whole(K, R), whole(R, K), whole(R, NJ)],
            out_specs=[out, out, whole(NJ, R), whole(K, R)],
            scratch_shapes=[pltpu.VMEM((K, R, NJ), F32)],
        ),
        out_shape=[jax.ShapeDtypeStruct((XL, Z, SHARD, R), F32)] * 2
        + [jax.ShapeDtypeStruct((NJ, R), F32), jax.ShapeDtypeStruct((K, R), F32)],
        compiler_params=pltpu.CompilerParams(vmem_limit_bytes=56 << 20),
        cost_estimate=pl.CostEstimate(flops=12_900_000_000, bytes_accessed=22_000_000, transcendentals=8_400_000),
        name="fused",
    )(table, target, target, target, target, a_all, b_full, c_half, c_half.T, b_full.T)


def on_device(target, a_factor, b_factor, c_factor):
    p = lax.axis_index("space")
    xl, z, core = p >> 3, (p >> 1) & 3, p & 1
    b_full = lax.all_to_all(jnp.broadcast_to(b_factor[None], (8, 64, R)), "samples", 0, 0).reshape(NJ, R)
    a_x = lax.ppermute(a_factor, "space", TO_XL)
    pair = jnp.concatenate([a_factor, a_x], axis=0)
    mine = [pair] + [lax.ppermute(pair, "space", from_z(d)) for d in (1, 2, 3)]
    theirs = [lax.ppermute(m, "space", TO_CORE) for m in mine]
    a_all = jnp.stack([jnp.concatenate([m, t], axis=0) for m, t in zip(mine, theirs)])
    dz, dc, dx = jnp.meshgrid(jnp.arange(4), jnp.arange(2), jnp.arange(2), indexing="ij")
    slots = ((xl ^ dx) * 8 + ((z + dz) & 3) * 2 + (core ^ dc)).reshape(16)
    table = jnp.concatenate([slots, xl[None], (z + jnp.arange(4)) & 3]).astype(jnp.int32)
    c_half = c_factor.astype(F32) * 0.5
    same, other, gb, gc = local(table, target.reshape(K, 16, SHARD, NJ), a_all, b_full, c_half)

    first = jnp.concatenate([gb.reshape(8, 64, R), jnp.broadcast_to(gc[None], (8, K, R))], axis=1)
    first = jnp.sum(lax.all_to_all(first, "samples", 0, 0), axis=0)
    grad_b, gc = first[:64], first[64:]
    gc = gc + lax.ppermute(gc, "space", TO_CORE)
    same = (same + lax.ppermute(other, "space", TO_CORE)).reshape(8, SHARD, R)
    second = jnp.concatenate([same, jnp.broadcast_to(gc[None], (8, K, R))], axis=1)
    second = jnp.sum(lax.all_to_all(second, "space", 0, 0, axis_index_groups=SAME_CORE), axis=0)
    return second[:SHARD], grad_b, second[SHARD:]


def solution(mesh):
    return jax.shard_map(
        on_device,
        mesh=mesh,
        in_specs=(
            P(None, "samples", "space"),
            P(("samples", "space"), None),
            P(("space", "samples"), None),
            P(),
        ),
        out_specs=(P(("samples", "space"), None), P(("space", "samples"), None), P()),
        check_vma=False,
    )
```

```python
import functools

import jax
import jax.numpy as jnp
from jax import lax
from jax.experimental import pallas as pl
from jax.experimental.pallas import tpu as pltpu
from jax.sharding import PartitionSpec as P

F32 = jnp.float32
BF16 = jnp.bfloat16
K, R = 8, 256
SHARD = 128
NB, NJ = 64, 512
XL, Z, CORE = 2, 4, 2
PEERS = 8

SPACE = range(XL * Z * CORE)
SAME_CORE = [[2 * g + c for g in range(XL * Z)] for c in range(CORE)]
TO_CORE = [(p, p ^ 1) for p in SPACE]
TO_XL = [(p, p ^ 8) for p in SPACE]


def from_z(d):
    return [((p & 9) | ((((p >> 1) + d) % 4) << 1), p) for p in SPACE]


def dot_last(x, y):
    return lax.dot_general(x, y, (((1,), (1,)), ((), ())), preferred_element_type=F32)


def add_up(x):
    return jnp.sum(x.astype(F32), axis=0)


def dot(x, y):
    return jnp.dot(x, y, preferred_element_type=F32)


def split(x):
    high = x.astype(BF16)
    return high, (x - high.astype(F32)).astype(BF16)


KH = 2


def body(last, place, t0, t1, t2, t3, *refs):
    n = 2 * (3 if last else 1)
    pieces, refs = refs[:n], refs[n:]
    b_any, c_ref, refs = refs[0], refs[1], refs[2:]
    if last:
        gb_in, gc_in, refs = refs[0], refs[1], refs[2:]
    same_ref, other_ref, *outs, w_ref, a_ref, b_ref, ch_ref, sems = refs
    step, part = pl.program_id(0), pl.program_id(1)

    def arrive(s, half):
        return pltpu.make_async_copy(pieces[2 * s + half], a_ref.at[s, pl.ds(half * 2 * SHARD, 2 * SHARD)], sems.at[2 * s + half])

    b_copy = pltpu.make_async_copy(b_any, b_ref, sems.at[n])

    @pl.when((step == 0) & (part == 0))
    def _():
        for s in range(n // 2):
            for half in range(2):
                arrive(s, half).start()
        b_copy.start()
        ch_ref[...] = c_ref[...].astype(F32) * 0.5
        for s in range(n // 2):
            for half in range(2):
                arrive(s, half).wait()
        b_copy.wait()

    rows = a_ref[step]
    wide = rows.astype(F32)
    rows_t = rows.T
    b = b_ref[...]
    grad = jnp.zeros((4 * SHARD, R), F32)
    for kk in range(K // KH):
        k = part * (K // KH) + kk
        ck = ch_ref[pl.ds(k, 1), :]
        half = dot_last((wide * ck).astype(BF16), b)
        t = jnp.concatenate([r[kk, 0] for r in (t0, t1, t2, t3)], axis=0).astype(F32)
        d2 = ((jnp.tanh(half) + 1.0) - (t + t)).astype(BF16)
        grad = grad + dot(d2, b) * ck
        w_ref[k] = jnp.where(step > 0, w_ref[k], 0.0) + dot(rows_t, d2)

    xl = place[0] >> 3
    for dx in range(2):
        at = lax.bitwise_xor(xl, dx)
        for slot, ref in ((dx, same_ref), (2 + dx, other_ref)):
            mine = grad[slot * SHARD : (slot + 1) * SHARD]
            ref[at, 0] = jnp.where(part > 0, ref[at, 0], 0.0) + mine

    @pl.when((step == pl.num_programs(0) - 1) & (part == KH - 1))
    def _():
        c_half = ch_ref[...]
        total = gb_in[...] if last else jnp.zeros((R, NJ), F32)
        lane = lax.broadcasted_iota(jnp.int32, (R, 128), 1)
        sums = jnp.zeros((R, 128), F32)
        bt = b_ref[...].T.astype(F32)
        c_t = jnp.concatenate([c_half, jnp.zeros((128 - K, R), F32)], axis=0).T
        for k in range(K):
            wk = w_ref[k]
            total = total + wk * c_t[:, k : k + 1]
            s = jnp.sum(wk * bt, axis=1, keepdims=True) * 0.5
            sums = jnp.where(lane == k, s, sums)
        if not last:
            outs[0][...] = total
            outs[1][...] = sums
            return
        grad_b = total.T.astype(BF16)
        high, low = split((sums + gc_in[...]).T[:K])
        for peer in range(PEERS):
            outs[0][peer, :NB] = grad_b[peer * NB : (peer + 1) * NB]
            outs[0][peer, NB:] = jnp.concatenate([high, low], axis=0)


def local(place, target, pieces, b_full, c_factor, *before):
    last = bool(before)
    steps, shift = (3, 1) if last else (1, 0)

    def tile(q):
        dc, dx = q // 2, q % 2

        def index(s, h, place):
            p = place[0]
            z = (lax.shift_right_logical(p, 1) + s + shift) & 3
            return h, ((p & 8) ^ (8 * dx)) + z * 2 + ((p & 1) ^ dc), 0, 0

        return pl.BlockSpec((K // KH, 1, SHARD, NJ), index)

    def whole(*shape):
        return pl.BlockSpec(shape, lambda s, h, place: (0,) * len(shape))

    anywhere = pl.BlockSpec(memory_space=pl.ANY)
    if last:
        out = pl.BlockSpec((XL, 1, SHARD, R), lambda s, h, place: (0, (lax.shift_right_logical(place[0], 1) + s + 1) & 3, 0, 0))
        after = [whole(PEERS, NB + 2 * K, R)]
        after_shape = [jax.ShapeDtypeStruct((PEERS, NB + 2 * K, R), BF16)]
        inputs = [whole(R, NJ), whole(R, 128)]
    else:
        out = pl.BlockSpec((XL, 1, SHARD, R), lambda s, h, place: (0, lax.shift_right_logical(place[0], 1) & 3, 0, 0))
        after = [whole(R, NJ), whole(R, 128)]
        after_shape = [jax.ShapeDtypeStruct((R, NJ), F32), jax.ShapeDtypeStruct((R, 128), F32)]
        inputs = []
    carried = [anywhere, anywhere] if last else []
    n = 2 * steps
    return pl.pallas_call(
        functools.partial(body if not last else skip_carried, last),
        grid_spec=pltpu.PrefetchScalarGridSpec(
            num_scalar_prefetch=1,
            grid=(steps, KH),
            in_specs=[tile(q) for q in range(4)] + [anywhere] * n + [anywhere, whole(K, R)] + inputs + carried,
            out_specs=[out, out] + after,
            scratch_shapes=[
                pltpu.VMEM((K, R, NJ), F32),
                pltpu.VMEM((steps, 4 * SHARD, R), BF16),
                pltpu.VMEM((NJ, R), BF16),
                pltpu.VMEM((K, R), F32),
                pltpu.SemaphoreType.DMA((n + 1,)),
            ],
        ),
        out_shape=[jax.ShapeDtypeStruct((XL, Z, SHARD, R), F32)] * 2 + after_shape,
        input_output_aliases={1 + 4 + n + 2 + 2: 0, 1 + 4 + n + 2 + 3: 1} if last else {},
        compiler_params=pltpu.CompilerParams(vmem_limit_bytes=46 << 20),
        cost_estimate=pl.CostEstimate(flops=3_230_000_000 * steps, bytes_accessed=5_500_000 * steps, transcendentals=2_100_000 * steps),
        name="rest" if last else "begin",
    )(place, target, target, target, target, *pieces, b_full, c_factor, *before)


def skip_carried(last, *refs):
    n = 1 + 4 + 6 + 2 + 2
    body(last, *refs[:n], *refs[n + 2 :])


def on_device(target, a_factor, b_factor, c_factor):
    place = lax.axis_index("space").astype(jnp.int32).reshape(1)
    b_full = lax.all_to_all(jnp.broadcast_to(b_factor[None], (PEERS, NB, R)), "samples", 0, 0).reshape(NJ, R)
    a_x = lax.ppermute(a_factor, "space", TO_XL)
    pair = jnp.concatenate([a_factor, a_x], axis=0)
    mine = [lax.ppermute(pair, "space", from_z(d)) if d else pair for d in range(Z)]
    target = target.reshape(K, 16, SHARD, NJ)
    same, other, gb, gc = local(place, target, [pair, lax.ppermute(pair, "space", TO_CORE)], b_full, c_factor)
    *mine, gc = lax.optimization_barrier((*mine[1:], gc))
    pieces = []
    for m in mine:
        pieces += [m, lax.ppermute(m, "space", TO_CORE)]
    same, other, first = local(place, target, pieces, b_full, c_factor, gb, gc, same, other)

    arrived = lax.ppermute(other, "space", TO_CORE)
    first = add_up(lax.all_to_all(first, "samples", 0, 0))
    grad_b, c_sum = first[:NB], first[NB : NB + K] + first[NB + K :]
    high, low = split(c_sum + lax.ppermute(c_sum, "space", TO_CORE))
    tail = jnp.broadcast_to(jnp.concatenate([high, low], axis=0)[None], (PEERS, 2 * K, R))
    second = (same + arrived).astype(BF16).reshape(PEERS, SHARD, R)
    second = lax.all_to_all(jnp.concatenate([second, tail], axis=1), "space", 0, 0, axis_index_groups=SAME_CORE)
    second = add_up(second)
    return second[:SHARD], grad_b, second[SHARD : SHARD + K] + second[SHARD + K :]


def solution(mesh):
    return jax.shard_map(
        on_device,
        mesh=mesh,
        in_specs=(
            P(None, "samples", "space"),
            P(("samples", "space"), None),
            P(("space", "samples"), None),
            P(),
        ),
        out_specs=(P(("samples", "space"), None), P(("space", "samples"), None), P()),
        check_vma=False,
    )
```

```python
import functools

import jax
import jax.numpy as jnp
from jax import lax
from jax.experimental import pallas as pl
from jax.experimental.pallas import tpu as pltpu
from jax.sharding import PartitionSpec as P

F32 = jnp.float32
BF16 = jnp.bfloat16
K, R = 8, 256
SHARD = 128
NB, NJ = 64, 512
XL, Z, CORE = 2, 4, 2
PEERS = 8

SPACE = range(XL * Z * CORE)
SAME_CORE = [[2 * g + c for g in range(XL * Z)] for c in range(CORE)]
TO_CORE = [(p, p ^ 1) for p in SPACE]
TO_XL = [(p, p ^ 8) for p in SPACE]


def from_z(d):
    return [((p & 9) | ((((p >> 1) + d) % 4) << 1), p) for p in SPACE]


def dot_last(x, y):
    return lax.dot_general(x, y, (((1,), (1,)), ((), ())), preferred_element_type=F32)


def add_up(x):
    return jnp.sum(x.astype(F32), axis=0)


def dot(x, y):
    return jnp.dot(x, y, preferred_element_type=F32)


def split(x):
    high = x.astype(BF16)
    return high, (x - high.astype(F32)).astype(BF16)


GROUP = 4 * SHARD
VMEM_LIMIT = 44 << 20


def body(last, place, t0, t1, t2, t3, *refs):
    steps = 3 if last else 1
    pieces, refs = refs[: 2 * steps], refs[2 * steps :]
    b_ref, c_ref, refs = refs[0], refs[1], refs[2:]
    if last:
        gb_in, gc_in, refs = refs[0], refs[1], refs[4:]
    same_ref, other_ref, *outs, w_ref, a_ref = refs
    step = pl.program_id(0)
    for s in range(steps):

        @pl.when(step == s)
        def _():
            a_ref[: 2 * SHARD] = pieces[2 * s][...]
            a_ref[2 * SHARD :] = pieces[2 * s + 1][...]

    rows = a_ref[...]
    wide = rows.astype(F32)
    rows_t = rows.T
    b = b_ref[...]
    c_half = c_ref[...]
    grad = jnp.zeros((GROUP, R), F32)
    for k in range(K):
        ck = c_half[k : k + 1, :]
        half = dot_last((wide * ck).astype(BF16), b)
        t = jnp.concatenate([r[k, 0] for r in (t0, t1, t2, t3)], axis=0).astype(F32)
        d2 = ((jnp.tanh(half) + 1.0) - (t + t)).astype(BF16)
        grad = grad + dot(d2, b) * ck
        part = dot(rows_t, d2)
        w_ref[k] = jnp.where(step > 0, w_ref[k], 0.0) + part if last else part

    xl = place[0] >> 3
    for dx in range(2):
        at = lax.bitwise_xor(xl, dx)
        same_ref[at, 0] = grad[dx * SHARD : (dx + 1) * SHARD]
        other_ref[at, 0] = grad[(2 + dx) * SHARD : (3 + dx) * SHARD]

    @pl.when(step == steps - 1)
    def _():
        total = gb_in[...] if last else jnp.zeros((R, NJ), F32)
        lane = lax.broadcasted_iota(jnp.int32, (R, 128), 1)
        sums = jnp.zeros((R, 128), F32)
        bt = b_ref[...].T.astype(F32)
        c_t = jnp.concatenate([c_half, jnp.zeros((128 - K, R), F32)], axis=0).T
        for k in range(K):
            wk = w_ref[k]
            total = total + wk * c_t[:, k : k + 1]
            s = jnp.sum(wk * bt, axis=1, keepdims=True) * 0.5
            sums = jnp.where(lane == k, s, sums)
        if not last:
            outs[0][...] = total
            outs[1][...] = sums
            return
        grad_b = total.T.astype(BF16)
        high, low = split((sums + gc_in[...]).T[:K])
        for peer in range(PEERS):
            outs[0][peer, :NB] = grad_b[peer * NB : (peer + 1) * NB]
            outs[0][peer, NB:] = jnp.concatenate([high, low], axis=0)


def local(place, target, pieces, b_full, c_half, *before):
    last = bool(before)
    steps, shift = (3, 1) if last else (1, 0)

    def tile(q):
        dc, dx = q // 2, q % 2

        def index(s, place):
            p = place[0]
            z = (lax.shift_right_logical(p, 1) + s + shift) & 3
            return 0, ((p & 8) ^ (8 * dx)) + z * 2 + ((p & 1) ^ dc), 0, 0

        return pl.BlockSpec((K, 1, SHARD, NJ), index)

    def whole(*shape):
        return pl.BlockSpec(shape, lambda s, place: (0,) * len(shape))

    anywhere = pl.BlockSpec(memory_space=pl.ANY)
    out = pl.BlockSpec(
        (XL, 1, SHARD, R), lambda s, place: (0, (lax.shift_right_logical(place[0], 1) + s + shift) & 3, 0, 0)
    )
    n = 2 * steps
    if last:
        after, carried = [((PEERS, NB + 2 * K, R), BF16)], [whole(R, NJ), whole(R, 128), anywhere, anywhere]
    else:
        after, carried = [((R, NJ), F32), ((R, 128), F32)], []
    return pl.pallas_call(
        functools.partial(body, last),
        grid_spec=pltpu.PrefetchScalarGridSpec(
            num_scalar_prefetch=1,
            grid=(steps,),
            in_specs=[tile(q) for q in range(4)] + [whole(2 * SHARD, R)] * n + [whole(NJ, R), whole(K, R)] + carried,
            out_specs=[out, out] + [whole(*shape) for shape, _ in after],
            scratch_shapes=[
                pltpu.VMEM((K, R, NJ), F32),
                pltpu.VMEM((GROUP, R), BF16),
            ],
        ),
        out_shape=[jax.ShapeDtypeStruct((XL, Z, SHARD, R), F32)] * 2
        + [jax.ShapeDtypeStruct(shape, dtype) for shape, dtype in after],
        input_output_aliases={n + 9: 0, n + 10: 1} if last else {},
        compiler_params=pltpu.CompilerParams(vmem_limit_bytes=VMEM_LIMIT),
        cost_estimate=pl.CostEstimate(
            flops=3_230_000_000 * steps, bytes_accessed=5_500_000 * steps, transcendentals=2_100_000 * steps
        ),
        name="rest" if last else "begin",
    )(place, target, target, target, target, *pieces, b_full, c_half, *before)


def on_device(target, a_factor, b_factor, c_factor):
    place = lax.axis_index("space").astype(jnp.int32).reshape(1)
    b_full = lax.all_to_all(jnp.broadcast_to(b_factor[None], (PEERS, NB, R)), "samples", 0, 0).reshape(NJ, R)
    c_half = c_factor.astype(F32) * 0.5
    a_x = lax.ppermute(a_factor, "space", TO_XL)
    pair = jnp.concatenate([a_factor, a_x], axis=0)
    mine = [lax.ppermute(pair, "space", from_z(d)) if d else pair for d in range(Z)]
    target = target.reshape(K, 16, SHARD, NJ)
    same, other, gb, gc = local(place, target, [pair, lax.ppermute(pair, "space", TO_CORE)], b_full, c_half)
    *mine, gc = lax.optimization_barrier((*mine[1:], gc))
    pieces = []
    for m in mine:
        pieces += [m, lax.ppermute(m, "space", TO_CORE)]
    same, other, first = local(place, target, pieces, b_full, c_half, gb, gc, same, other)

    arrived = lax.ppermute(other, "space", TO_CORE)
    first = add_up(lax.all_to_all(first, "samples", 0, 0))
    grad_b, c_sum = first[:NB], first[NB : NB + K] + first[NB + K :]
    high, low = split(c_sum + lax.ppermute(c_sum, "space", TO_CORE))
    tail = jnp.broadcast_to(jnp.concatenate([high, low], axis=0)[None], (PEERS, 2 * K, R))
    second = (same + arrived).astype(BF16).reshape(PEERS, SHARD, R)
    second = lax.all_to_all(jnp.concatenate([second, tail], axis=1), "space", 0, 0, axis_index_groups=SAME_CORE)
    second = add_up(second)
    return second[:SHARD], grad_b, second[SHARD : SHARD + K] + second[SHARD + K :]


def solution(mesh):
    return jax.shard_map(
        on_device,
        mesh=mesh,
        in_specs=(
            P(None, "samples", "space"),
            P(("samples", "space"), None),
            P(("space", "samples"), None),
            P(),
        ),
        out_specs=(P(("samples", "space"), None), P(("space", "samples"), None), P()),
        check_vma=False,
    )
```

```python
import functools

import jax
import jax.numpy as jnp
from jax import lax
from jax.experimental import pallas as pl
from jax.experimental.pallas import tpu as pltpu
from jax.sharding import PartitionSpec as P

F32 = jnp.float32
BF16 = jnp.bfloat16
K, R = 8, 256
SHARD = 128
NB, NJ = 64, 512
XL, Z, CORE = 2, 4, 2
PEERS = 8

SPACE = range(XL * Z * CORE)
TO_CORE = [(p, p ^ 1) for p in SPACE]
TO_XL = [(p, p ^ 8) for p in SPACE]


def from_z(d):
    return [((p & 9) | ((((p >> 1) + d) % 4) << 1), p) for p in SPACE]


def dot_last(x, y):
    return lax.dot_general(x, y, (((1,), (1,)), ((), ())), preferred_element_type=F32)


def dot(x, y):
    return jnp.dot(x, y, preferred_element_type=F32)


def split(x):
    high = x.astype(BF16)
    return high, (x - high.astype(F32)).astype(BF16)


GROUP = 4 * SHARD
VMEM_LIMIT = 44 << 20


def body(last, place, t0, t1, t2, t3, *refs):
    steps = 3 if last else 1
    pieces, refs = refs[: 2 * steps], refs[2 * steps :]
    b_ref, c_ref, refs = refs[0], refs[1], refs[2:]
    if last:
        gb_in, gc_in, refs = refs[0], refs[1], refs[6:]
    parts, outs, w_ref, a_ref = refs[:4], refs[4:-2], refs[-2], refs[-1]
    step = pl.program_id(0)
    for s in range(steps):

        @pl.when(step == s)
        def _():
            a_ref[: 2 * SHARD] = pieces[2 * s][...]
            a_ref[2 * SHARD :] = pieces[2 * s + 1][...]

    rows = a_ref[...]
    wide = rows.astype(F32)
    rows_t = rows.T
    b = b_ref[...]
    c_half = c_ref[...]
    grad = jnp.zeros((GROUP, R), F32)
    for k in range(K):
        ck = c_half[k : k + 1, :]
        half = dot_last((wide * ck).astype(BF16), b)
        t = jnp.concatenate([r[k, 0] for r in (t0, t1, t2, t3)], axis=0).astype(F32)
        d2 = ((jnp.tanh(half) + 1.0) - (t + t)).astype(BF16)
        grad = grad + dot(d2, b) * ck
        part = dot(rows_t, d2)
        w_ref[k] = jnp.where(step > 0, w_ref[k], 0.0) + part if last else part

    for slot in range(4):
        parts[slot][0] = grad[slot * SHARD : (slot + 1) * SHARD]

    @pl.when(step == steps - 1)
    def _():
        total = gb_in[...] if last else jnp.zeros((R, NJ), F32)
        lane = lax.broadcasted_iota(jnp.int32, (R, 128), 1)
        sums = jnp.zeros((R, 128), F32)
        bt = b_ref[...].T.astype(F32)
        c_t = jnp.concatenate([c_half, jnp.zeros((128 - K, R), F32)], axis=0).T
        for k in range(K):
            wk = w_ref[k]
            total = total + wk * c_t[:, k : k + 1]
            s = jnp.sum(wk * bt, axis=1, keepdims=True) * 0.5
            sums = jnp.where(lane == k, s, sums)
        if not last:
            outs[0][...] = total
            outs[1][...] = sums
            return
        grad_b = total.T.astype(BF16)
        high, low = split((sums + gc_in[...]).T[:K])
        outs[0][...] = grad_b
        for peer in range(XL * Z * CORE):
            outs[1][peer] = jnp.concatenate([high, low], axis=0)


def local(place, target, pieces, b_full, c_half, *before):
    last = bool(before)
    steps, shift = (3, 1) if last else (1, 0)

    def tile(q):
        dc, dx = q // 2, q % 2

        def index(s, place):
            p = place[0]
            z = (lax.shift_right_logical(p, 1) + s + shift) & 3
            return 0, ((p & 8) ^ (8 * dx)) + z * 2 + ((p & 1) ^ dc), 0, 0

        return pl.BlockSpec((K, 1, SHARD, NJ), index)

    def whole(*shape):
        return pl.BlockSpec(shape, lambda s, place: (0,) * len(shape))

    anywhere = pl.BlockSpec(memory_space=pl.ANY)
    out = pl.BlockSpec((1, SHARD, R), lambda s, place: (s + shift, 0, 0))
    n = 2 * steps
    if last:
        after, carried = [((NJ, R), BF16), ((XL * Z * CORE, 2 * K, R), BF16)], [whole(R, NJ), whole(R, 128)] + [anywhere] * 4
    else:
        after, carried = [((R, NJ), F32), ((R, 128), F32)], []
    return pl.pallas_call(
        functools.partial(body, last),
        grid_spec=pltpu.PrefetchScalarGridSpec(
            num_scalar_prefetch=1,
            grid=(steps,),
            in_specs=[tile(q) for q in range(4)] + [whole(2 * SHARD, R)] * n + [whole(NJ, R), whole(K, R)] + carried,
            out_specs=[out] * 4 + [whole(*shape) for shape, _ in after],
            scratch_shapes=[
                pltpu.VMEM((K, R, NJ), F32),
                pltpu.VMEM((GROUP, R), BF16),
            ],
        ),
        out_shape=[jax.ShapeDtypeStruct((Z, SHARD, R), F32)] * 4
        + [jax.ShapeDtypeStruct(shape, dtype) for shape, dtype in after],
        input_output_aliases={n + 9 + i: i for i in range(4)} if last else {},
        compiler_params=pltpu.CompilerParams(vmem_limit_bytes=VMEM_LIMIT),
        cost_estimate=pl.CostEstimate(
            flops=3_230_000_000 * steps, bytes_accessed=5_500_000 * steps, transcendentals=2_100_000 * steps
        ),
        name="rest" if last else "begin",
    )(place, target, target, target, target, *pieces, b_full, c_half, *before)


def total(ref, first, rows):
    out = ref[0, first : first + rows].astype(F32)
    for peer in range(1, ref.shape[0]):
        out = out + ref[peer, first : first + rows].astype(F32)
    return out


def small(body, name, *out_shape):
    shapes = [jax.ShapeDtypeStruct(shape, dtype) for shape, dtype in out_shape]
    return pl.pallas_call(body, out_shape=shapes, compiler_params=pltpu.CompilerParams(vmem_limit_bytes=8 << 20), name=name)


def join(x_ref, y_ref, out_ref):
    out_ref[...] = (x_ref[...] + y_ref[...]).astype(BF16)


def pack(times_ref, gb_ref, out_ref):
    high, low = split(total(times_ref, 0, K) + total(times_ref, K, K))
    tail = jnp.concatenate([high, low], axis=0)
    for peer in range(PEERS):
        out_ref[peer, :NB] = gb_ref[peer * NB : (peer + 1) * NB]
        out_ref[peer, NB:] = tail


def spread(x_ref, y_ref, across_ref, own_ref, *out_refs):
    own_ref[...] = x_ref[0] + y_ref[0] + across_ref[0].astype(F32)
    for d, ref in enumerate(out_refs, 1):
        ref[...] = (x_ref[d] + y_ref[d] + across_ref[d].astype(F32)).astype(BF16)


def finish(first_ref, own_ref, g1, g2, g3, grad_a, grad_b, grad_c):
    grad_a[...] = own_ref[...] + g1[...].astype(F32) + g2[...].astype(F32) + g3[...].astype(F32)
    grad_b[...] = total(first_ref, 0, NB)
    grad_c[...] = total(first_ref, NB, K) + total(first_ref, NB + K, K)


def on_device(target, a_factor, b_factor, c_factor):
    place = lax.axis_index("space").astype(jnp.int32).reshape(1)
    b_full = lax.all_to_all(jnp.broadcast_to(b_factor[None], (PEERS, NB, R)), "samples", 0, 0).reshape(NJ, R)
    c_half = c_factor.astype(F32) * 0.5
    a_x = lax.ppermute(a_factor, "space", TO_XL)
    pair = jnp.concatenate([a_factor, a_x], axis=0)
    mine = [lax.ppermute(pair, "space", from_z(d)) if d else pair for d in range(Z)]
    target = target.reshape(K, 16, SHARD, NJ)
    *parts, gb, gc = local(place, target, [pair, lax.ppermute(pair, "space", TO_CORE)], b_full, c_half)
    *mine, gc = lax.optimization_barrier((*mine[1:], gc))
    pieces = []
    for m in mine:
        pieces += [m, lax.ppermute(m, "space", TO_CORE)]
    own, far, own_core, far_core, first, times = local(place, target, pieces, b_full, c_half, gb, gc, *parts)

    far_core = lax.ppermute(far_core, "space", TO_CORE)
    own_core = lax.ppermute(own_core, "space", TO_CORE)
    times = lax.all_to_all(times, "space", 0, 0)
    (across,) = small(join, "join", ((Z, SHARD, R), BF16))(far, far_core)
    across = lax.ppermute(across, "space", TO_XL)
    times, across = lax.optimization_barrier((times, across))
    (first,) = small(pack, "pack", ((PEERS, NB + 2 * K, R), BF16))(times, first)
    first = lax.all_to_all(first, "samples", 0, 0)
    piece = (SHARD, R)
    own, *away = small(spread, "spread", (piece, F32), *[(piece, BF16)] * 3)(own, own_core, across)
    away = [lax.ppermute(x, "space", from_z(-d)) for d, x in enumerate(away, 1)]
    first, *away = lax.optimization_barrier((first, *away))
    return tuple(small(finish, "finish", (piece, F32), ((NB, R), F32), ((K, R), F32))(first, own, *away))


def solution(mesh):
    return jax.shard_map(
        on_device,
        mesh=mesh,
        in_specs=(
            P(None, "samples", "space"),
            P(("samples", "space"), None),
            P(("space", "samples"), None),
            P(),
        ),
        out_specs=(P(("samples", "space"), None), P(("space", "samples"), None), P()),
        check_vma=False,
    )
```

```python
import functools

import jax
import jax.numpy as jnp
from jax import lax
from jax.experimental import pallas as pl
from jax.experimental.pallas import tpu as pltpu
from jax.sharding import PartitionSpec as P

F32 = jnp.float32
BF16 = jnp.bfloat16
K, R = 8, 256
SHARD = 128
NB, NJ = 64, 512
XL, Z, CORE = 2, 4, 2
PEERS = 8

SPACE = range(XL * Z * CORE)
TO_CORE = [(p, p ^ 1) for p in SPACE]
TO_XL = [(p, p ^ 8) for p in SPACE]


def from_z(d):
    return [((p & 9) | ((((p >> 1) + d) % 4) << 1), p) for p in SPACE]


def dot_last(x, y):
    return lax.dot_general(x, y, (((1,), (1,)), ((), ())), preferred_element_type=F32)


def dot(x, y):
    return jnp.dot(x, y, preferred_element_type=F32)


def split(x):
    high = x.astype(BF16)
    return high, (x - high.astype(F32)).astype(BF16)


GROUP = 4 * SHARD
VMEM_LIMIT = 44 << 20


def body(last, place, t0, t1, t2, t3, *refs):
    steps = 3 if last else 1
    mine, theirs, refs = refs[0], refs[1], refs[2:]
    b_ref, c_ref, refs = refs[0], refs[1], refs[2:]
    if last:
        gb_in, gc_in, refs = refs[0], refs[1], refs[6:]
    parts, outs, w_ref, a_ref = refs[:4], refs[4:-2], refs[-2], refs[-1]
    step = pl.program_id(0)
    a_ref[: 2 * SHARD] = mine[step]
    a_ref[2 * SHARD :] = theirs[step]
    rows = a_ref[...]
    wide = rows.astype(F32)
    rows_t = rows.T
    b = b_ref[...]
    c_half = c_ref[...]
    grad = jnp.zeros((GROUP, R), F32)
    for k in range(K):
        ck = c_half[k : k + 1, :]
        half = dot_last((wide * ck).astype(BF16), b)
        t = jnp.concatenate([r[k, 0] for r in (t0, t1, t2, t3)], axis=0).astype(F32)
        d2 = ((jnp.tanh(half) + 1.0) - (t + t)).astype(BF16)
        grad = grad + dot(d2, b) * ck
        part = dot(rows_t, d2)
        w_ref[k] = jnp.where(step > 0, w_ref[k], 0.0) + part if last else part

    for slot in range(4):
        parts[slot][0] = grad[slot * SHARD : (slot + 1) * SHARD]

    @pl.when(step == steps - 1)
    def _():
        total = gb_in[...] if last else jnp.zeros((R, NJ), F32)
        lane = lax.broadcasted_iota(jnp.int32, (R, 128), 1)
        sums = jnp.zeros((R, 128), F32)
        bt = b_ref[...].T.astype(F32)
        c_t = jnp.concatenate([c_half, jnp.zeros((128 - K, R), F32)], axis=0).T
        for k in range(K):
            wk = w_ref[k]
            total = total + wk * c_t[:, k : k + 1]
            s = jnp.sum(wk * bt, axis=1, keepdims=True) * 0.5
            sums = jnp.where(lane == k, s, sums)
        if not last:
            outs[0][...] = total
            outs[1][...] = sums
            return
        grad_b = total.T.astype(BF16)
        high, low = split((sums + gc_in[...]).T[:K])
        outs[0][...] = grad_b
        for peer in range(XL * Z * CORE):
            outs[1][peer] = jnp.concatenate([high, low], axis=0)


def local(place, target, pieces, b_full, c_half, *before):
    last = bool(before)
    steps, shift = (3, 1) if last else (1, 0)

    def tile(q):
        dc, dx = q // 2, q % 2

        def index(s, place):
            p = place[0]
            z = (lax.shift_right_logical(p, 1) + s + shift) & 3
            return 0, ((p & 8) ^ (8 * dx)) + z * 2 + ((p & 1) ^ dc), 0, 0

        return pl.BlockSpec((K, 1, SHARD, NJ), index)

    def whole(*shape):
        return pl.BlockSpec(shape, lambda s, place: (0,) * len(shape))

    anywhere = pl.BlockSpec(memory_space=pl.ANY)
    out = pl.BlockSpec((1, SHARD, R), lambda s, place: (s + shift, 0, 0))
    if last:
        after, carried = [((NJ, R), BF16), ((XL * Z * CORE, 2 * K, R), BF16)], [whole(R, NJ), whole(R, 128)] + [anywhere] * 4
    else:
        after, carried = [((R, NJ), F32), ((R, 128), F32)], []
    return pl.pallas_call(
        functools.partial(body, last),
        grid_spec=pltpu.PrefetchScalarGridSpec(
            num_scalar_prefetch=1,
            grid=(steps,),
            in_specs=[tile(q) for q in range(4)] + [whole(steps, 2 * SHARD, R)] * 2 + [whole(NJ, R), whole(K, R)] + carried,
            out_specs=[out] * 4 + [whole(*shape) for shape, _ in after],
            scratch_shapes=[
                pltpu.VMEM((K, R, NJ), F32),
                pltpu.VMEM((GROUP, R), BF16),
            ],
        ),
        out_shape=[jax.ShapeDtypeStruct((Z, SHARD, R), F32)] * 4
        + [jax.ShapeDtypeStruct(shape, dtype) for shape, dtype in after],
        input_output_aliases={11 + i: i for i in range(4)} if last else {},
        compiler_params=pltpu.CompilerParams(vmem_limit_bytes=VMEM_LIMIT),
        cost_estimate=pl.CostEstimate(
            flops=3_230_000_000 * steps, bytes_accessed=5_500_000 * steps, transcendentals=2_100_000 * steps
        ),
        name="rest" if last else "begin",
    )(place, target, target, target, target, *pieces, b_full, c_half, *before)


def total(ref, first, rows):
    out = ref[0, first : first + rows].astype(F32)
    for peer in range(1, ref.shape[0]):
        out = out + ref[peer, first : first + rows].astype(F32)
    return out


def small(body, name, *out_shape):
    shapes = [jax.ShapeDtypeStruct(shape, dtype) for shape, dtype in out_shape]
    return pl.pallas_call(body, out_shape=shapes, compiler_params=pltpu.CompilerParams(vmem_limit_bytes=8 << 20), name=name)


def repeat(x_ref, out_ref):
    for peer in range(PEERS):
        out_ref[peer] = x_ref[...]


def stack(*refs):
    for i, ref in enumerate(refs[:-1]):
        refs[-1][i] = ref[...]


def join(x_ref, y_ref, out_ref):
    out_ref[...] = (x_ref[...] + y_ref[...]).astype(BF16)


def pack(times_ref, gb_ref, out_ref):
    high, low = split(total(times_ref, 0, K) + total(times_ref, K, K))
    tail = jnp.concatenate([high, low], axis=0)
    for peer in range(PEERS):
        out_ref[peer, :NB] = gb_ref[peer * NB : (peer + 1) * NB]
        out_ref[peer, NB:] = tail


def spread(x_ref, y_ref, across_ref, own_ref, *out_refs):
    own_ref[...] = x_ref[0] + y_ref[0] + across_ref[0].astype(F32)
    for d, ref in enumerate(out_refs, 1):
        ref[...] = (x_ref[d] + y_ref[d] + across_ref[d].astype(F32)).astype(BF16)


def finish(first_ref, own_ref, g1, g2, g3, grad_a, grad_b, grad_c):
    grad_a[...] = own_ref[...] + g1[...].astype(F32) + g2[...].astype(F32) + g3[...].astype(F32)
    grad_b[...] = total(first_ref, 0, NB)
    grad_c[...] = total(first_ref, NB, K) + total(first_ref, NB + K, K)


def on_device(target, a_factor, b_factor, c_factor):
    place = lax.axis_index("space").astype(jnp.int32).reshape(1)
    (b_wide,) = small(repeat, "repeat", ((PEERS, NB, R), BF16))(b_factor)
    b_full = lax.all_to_all(b_wide, "samples", 0, 0).reshape(NJ, R)
    c_half = c_factor.astype(F32) * 0.5
    a_x = lax.ppermute(a_factor, "space", TO_XL)
    pair = jnp.concatenate([a_factor, a_x], axis=0)
    mine = [lax.ppermute(pair, "space", from_z(d)) if d else pair for d in range(Z)]
    target = target.reshape(K, 16, SHARD, NJ)
    *parts, gb, gc = local(place, target, [pair[None], lax.ppermute(pair, "space", TO_CORE)[None]], b_full, c_half)
    *mine, gc = lax.optimization_barrier((*mine[1:], gc))
    (mine,) = small(stack, "stack", ((Z - 1, 2 * SHARD, R), BF16))(*mine)
    pieces = [mine, lax.ppermute(mine, "space", TO_CORE)]
    own, far, own_core, far_core, first, times = local(place, target, pieces, b_full, c_half, gb, gc, *parts)

    far_core = lax.ppermute(far_core, "space", TO_CORE)
    own_core = lax.ppermute(own_core, "space", TO_CORE)
    times = lax.all_to_all(times, "space", 0, 0)
    times, far_core = lax.optimization_barrier((times, far_core))
    (across,) = small(join, "join", ((Z, SHARD, R), BF16))(far, far_core)
    across = lax.ppermute(across, "space", TO_XL)
    (first,) = small(pack, "pack", ((PEERS, NB + 2 * K, R), BF16))(times, first)
    first = lax.all_to_all(first, "samples", 0, 0)
    piece = (SHARD, R)
    own, *away = small(spread, "spread", (piece, F32), *[(piece, BF16)] * 3)(own, own_core, across)
    away = [lax.ppermute(x, "space", from_z(-d)) for d, x in enumerate(away, 1)]
    first, *away = lax.optimization_barrier((first, *away))
    return tuple(small(finish, "finish", (piece, F32), ((NB, R), F32), ((K, R), F32))(first, own, *away))


def solution(mesh):
    return jax.shard_map(
        on_device,
        mesh=mesh,
        in_specs=(
            P(None, "samples", "space"),
            P(("samples", "space"), None),
            P(("space", "samples"), None),
            P(),
        ),
        out_specs=(P(("samples", "space"), None), P(("space", "samples"), None), P()),
        check_vma=False,
    )
```

```python
import functools

import jax
import jax.numpy as jnp
from jax import lax
from jax.experimental import pallas as pl
from jax.experimental.pallas import tpu as pltpu
from jax.sharding import PartitionSpec as P

F32 = jnp.float32
BF16 = jnp.bfloat16
K, R = 8, 256
SHARD = 128
NB, NJ = 64, 512
XL, Z, CORE = 2, 4, 2
PEERS = 8
AWAY = 2, 1, 3

SPACE = range(XL * Z * CORE)
TO_CORE = [(p, p ^ 1) for p in SPACE]
TO_XL = [(p, p ^ 8) for p in SPACE]


def from_z(d):
    return [((p & 9) | ((((p >> 1) + d) % 4) << 1), p) for p in SPACE]


def dot_last(x, y):
    return lax.dot_general(x, y, (((1,), (1,)), ((), ())), preferred_element_type=F32)


def dot(x, y):
    return jnp.dot(x, y, preferred_element_type=F32)


def split(x):
    high = x.astype(BF16)
    return high, (x - high.astype(F32)).astype(BF16)


GROUP = 4 * SHARD
VMEM_LIMIT = 44 << 20


def body(last, place, t0, t1, t2, t3, *refs):
    steps = 3 if last else 1
    mine, theirs, refs = refs[0], refs[1], refs[2:]
    b_ref, c_ref, refs = refs[0], refs[1], refs[2:]
    if last:
        gb_in, gc_in, refs = refs[0], refs[1], refs[6:]
    parts, outs, w_ref, a_ref = refs[:4], refs[4:-2], refs[-2], refs[-1]
    step = pl.program_id(0)
    a_ref[: 2 * SHARD] = mine[step]
    a_ref[2 * SHARD :] = theirs[step]
    rows = a_ref[...]
    wide = rows.astype(F32)
    rows_t = rows.T
    b = b_ref[...]
    c_half = c_ref[...]
    grad = jnp.zeros((GROUP, R), F32)
    for k in range(K):
        ck = c_half[k : k + 1, :]
        half = dot_last((wide * ck).astype(BF16), b)
        t = jnp.concatenate([r[k, 0] for r in (t0, t1, t2, t3)], axis=0).astype(F32)
        d2 = ((jnp.tanh(half) + 1.0) - (t + t)).astype(BF16)
        grad = grad + dot(d2, b) * ck
        part = dot(rows_t, d2)
        w_ref[k] = jnp.where(step > 0, w_ref[k], 0.0) + part if last else part

    for slot in range(4):
        parts[slot][0] = grad[slot * SHARD : (slot + 1) * SHARD]

    @pl.when(step == steps - 1)
    def _():
        total = gb_in[...] if last else jnp.zeros((R, NJ), F32)
        lane = lax.broadcasted_iota(jnp.int32, (R, 128), 1)
        sums = jnp.zeros((R, 128), F32)
        bt = b_ref[...].T.astype(F32)
        c_t = jnp.concatenate([c_half, jnp.zeros((128 - K, R), F32)], axis=0).T
        for k in range(K):
            wk = w_ref[k]
            total = total + wk * c_t[:, k : k + 1]
            s = jnp.sum(wk * bt, axis=1, keepdims=True) * 0.5
            sums = jnp.where(lane == k, s, sums)
        if not last:
            outs[0][...] = total
            outs[1][...] = sums
            return
        grad_b = total.T.astype(BF16)
        high, low = split((sums + gc_in[...]).T[:K])
        outs[0][...] = grad_b
        for peer in range(XL * Z * CORE):
            outs[1][peer] = jnp.concatenate([high, low], axis=0)


def local(place, target, pieces, b_full, c_half, *before):
    last = bool(before)
    steps, shift = (3, 1) if last else (1, 0)

    def tile(q):
        dc, dx = q // 2, q % 2

        def index(s, place):
            p = place[0]
            z = (lax.shift_right_logical(p, 1) + s + shift) & 3
            return 0, ((p & 8) ^ (8 * dx)) + z * 2 + ((p & 1) ^ dc), 0, 0

        return pl.BlockSpec((K, 1, SHARD, NJ), index)

    def whole(*shape):
        return pl.BlockSpec(shape, lambda s, place: (0,) * len(shape))

    anywhere = pl.BlockSpec(memory_space=pl.ANY)
    out = pl.BlockSpec((1, SHARD, R), lambda s, place: (s + shift, 0, 0))
    if last:
        after, carried = [((NJ, R), BF16), ((XL * Z * CORE, 2 * K, R), BF16)], [whole(R, NJ), whole(R, 128)] + [anywhere] * 4
    else:
        after, carried = [((R, NJ), F32), ((R, 128), F32)], []
    return pl.pallas_call(
        functools.partial(body, last),
        grid_spec=pltpu.PrefetchScalarGridSpec(
            num_scalar_prefetch=1,
            grid=(steps,),
            in_specs=[tile(q) for q in range(4)] + [whole(steps, 2 * SHARD, R)] * 2 + [whole(NJ, R), whole(K, R)] + carried,
            out_specs=[out] * 4 + [whole(*shape) for shape, _ in after],
            scratch_shapes=[
                pltpu.VMEM((K, R, NJ), F32),
                pltpu.VMEM((GROUP, R), BF16),
            ],
        ),
        out_shape=[jax.ShapeDtypeStruct((Z, SHARD, R), F32)] * 4
        + [jax.ShapeDtypeStruct(shape, dtype) for shape, dtype in after],
        input_output_aliases={11 + i: i for i in range(4)} if last else {},
        compiler_params=pltpu.CompilerParams(vmem_limit_bytes=VMEM_LIMIT),
        cost_estimate=pl.CostEstimate(
            flops=3_230_000_000 * steps, bytes_accessed=5_500_000 * steps, transcendentals=2_100_000 * steps
        ),
        name="rest" if last else "begin",
    )(place, target, target, target, target, *pieces, b_full, c_half, *before)


def total(ref, first, rows):
    out = ref[0, first : first + rows].astype(F32)
    for peer in range(1, ref.shape[0]):
        out = out + ref[peer, first : first + rows].astype(F32)
    return out


def small(body, name, *out_shape, room=8):
    shapes = [jax.ShapeDtypeStruct(shape, dtype) for shape, dtype in out_shape]
    return pl.pallas_call(body, out_shape=shapes, compiler_params=pltpu.CompilerParams(vmem_limit_bytes=room << 20), name=name)


def repeat(x_ref, out_ref):
    for peer in range(PEERS):
        out_ref[peer] = x_ref[...]


def stack(*refs):
    for i, ref in enumerate(refs[:-1]):
        refs[-1][i] = ref[...]


def join(x_ref, y_ref, out_ref):
    out_ref[...] = (x_ref[...] + y_ref[...]).astype(BF16)


def pack(times_ref, gb_ref, out_ref):
    high, low = split(total(times_ref, 0, K) + total(times_ref, K, K))
    tail = jnp.concatenate([high, low], axis=0)
    for peer in range(PEERS):
        out_ref[peer, :NB] = gb_ref[peer * NB : (peer + 1) * NB]
        out_ref[peer, NB:] = tail


def spread(x_ref, y_ref, across_ref, own_ref, *out_refs):
    own_ref[...] = x_ref[0] + y_ref[0] + across_ref[0].astype(F32)
    for d, ref in zip(AWAY, out_refs):
        ref[...] = (x_ref[d] + y_ref[d] + across_ref[d].astype(F32)).astype(BF16)


def finish(first_ref, own_ref, g1, g2, g3, grad_a, grad_b, grad_c):
    grad_a[...] = own_ref[...] + g1[...].astype(F32) + g2[...].astype(F32) + g3[...].astype(F32)
    grad_b[...] = total(first_ref, 0, NB)
    grad_c[...] = total(first_ref, NB, K) + total(first_ref, NB + K, K)


def on_device(target, a_factor, b_factor, c_factor):
    place = lax.axis_index("space").astype(jnp.int32).reshape(1)
    (b_wide,) = small(repeat, "repeat", ((PEERS, NB, R), BF16), room=60)(b_factor)
    b_full = lax.all_to_all(b_wide, "samples", 0, 0).reshape(NJ, R)
    c_half = c_factor.astype(F32) * 0.5
    a_x = lax.ppermute(a_factor, "space", TO_XL)
    pair = jnp.concatenate([a_factor, a_x], axis=0)
    mine = [lax.ppermute(pair, "space", from_z(d)) if d else pair for d in range(Z)]
    target = target.reshape(K, 16, SHARD, NJ)
    *parts, gb, gc = local(place, target, [pair[None], lax.ppermute(pair, "space", TO_CORE)[None]], b_full, c_half)
    *mine, gc = lax.optimization_barrier((*mine[1:], gc))
    (mine,) = small(stack, "stack", ((Z - 1, 2 * SHARD, R), BF16))(*mine)
    pieces = [mine, lax.ppermute(mine, "space", TO_CORE)]
    own, far, own_core, far_core, first, times = local(place, target, pieces, b_full, c_half, gb, gc, *parts)

    far_core = lax.ppermute(far_core, "space", TO_CORE)
    own_core = lax.ppermute(own_core, "space", TO_CORE)
    times = lax.all_to_all(times, "space", 0, 0)
    times, far_core = lax.optimization_barrier((times, far_core))
    (across,) = small(join, "join", ((Z, SHARD, R), BF16))(far, far_core)
    across = lax.ppermute(across, "space", TO_XL)
    (first,) = small(pack, "pack", ((PEERS, NB + 2 * K, R), BF16))(times, first)
    first = lax.all_to_all(first, "samples", 0, 0)
    piece = (SHARD, R)
    own, *away = small(spread, "spread", (piece, F32), *[(piece, BF16)] * 3)(own, own_core, across)
    away = [lax.ppermute(x, "space", from_z(-d)) for d, x in zip(AWAY, away)]
    first, *away = lax.optimization_barrier((first, *away))
    return tuple(small(finish, "finish", (piece, F32), ((NB, R), F32), ((K, R), F32))(first, own, *away))


def solution(mesh):
    return jax.shard_map(
        on_device,
        mesh=mesh,
        in_specs=(
            P(None, "samples", "space"),
            P(("samples", "space"), None),
            P(("space", "samples"), None),
            P(),
        ),
        out_specs=(P(("samples", "space"), None), P(("space", "samples"), None), P()),
        check_vma=False,
    )
```

```python
import functools

import jax
import jax.numpy as jnp
from jax import lax
from jax.experimental import pallas as pl
from jax.experimental.pallas import tpu as pltpu
from jax.sharding import PartitionSpec as P

F32 = jnp.float32
BF16 = jnp.bfloat16
K, R = 8, 256
SHARD = 128
NB, NJ = 64, 512
XL, Z, CORE = 2, 4, 2
PEERS = 8
AWAY = 2, 1, 3

SPACE = range(XL * Z * CORE)
TO_CORE = [(p, p ^ 1) for p in SPACE]
TO_XL = [(p, p ^ 8) for p in SPACE]


def from_z(d):
    return [((p & 9) | ((((p >> 1) + d) % 4) << 1), p) for p in SPACE]


def dot_last(x, y):
    return lax.dot_general(x, y, (((1,), (1,)), ((), ())), preferred_element_type=F32)


def dot(x, y):
    return jnp.dot(x, y, preferred_element_type=F32)


def split(x):
    high = x.astype(BF16)
    return high, (x - high.astype(F32)).astype(BF16)


GROUP = 4 * SHARD
VMEM_LIMIT = 44 << 20


def body(last, place, t0, t1, t2, t3, *refs):
    steps = 3 if last else 1
    mine, theirs, refs = refs[0], refs[1], refs[2:]
    b_ref, refs = refs[0], refs[1:]
    if last:
        gb_in, gc_in, refs = refs[0], refs[1], refs[6:]
    parts, outs, w_ref, a_ref = refs[:4], refs[4:-2], refs[-2], refs[-1]
    step = pl.program_id(0)
    a_ref[: 2 * SHARD] = mine[step]
    a_ref[2 * SHARD :] = theirs[step]
    rows = a_ref[...]
    wide = rows.astype(F32)
    rows_t = rows.T
    b = jnp.concatenate([b_ref[peer, :NB] for peer in range(PEERS)], axis=0)
    c_half = b_ref[0, NB : NB + K].astype(F32) * 0.5
    grad = jnp.zeros((GROUP, R), F32)
    for k in range(K):
        ck = c_half[k : k + 1, :]
        half = dot_last((wide * ck).astype(BF16), b)
        t = jnp.concatenate([r[k, 0] for r in (t0, t1, t2, t3)], axis=0).astype(F32)
        d2 = ((jnp.tanh(half) + 1.0) - (t + t)).astype(BF16)
        grad = grad + dot(d2, b) * ck
        part = dot(rows_t, d2)
        w_ref[k] = jnp.where(step > 0, w_ref[k], 0.0) + part if last else part

    for slot in range(4):
        parts[slot][0] = grad[slot * SHARD : (slot + 1) * SHARD]

    @pl.when(step == steps - 1)
    def _():
        total = gb_in[...] if last else jnp.zeros((R, NJ), F32)
        lane = lax.broadcasted_iota(jnp.int32, (R, 128), 1)
        sums = jnp.zeros((R, 128), F32)
        bt = b.T.astype(F32)
        c_t = jnp.concatenate([c_half, jnp.zeros((128 - K, R), F32)], axis=0).T
        for k in range(K):
            wk = w_ref[k]
            total = total + wk * c_t[:, k : k + 1]
            s = jnp.sum(wk * bt, axis=1, keepdims=True) * 0.5
            sums = jnp.where(lane == k, s, sums)
        if not last:
            outs[0][...] = total
            outs[1][...] = sums
            return
        grad_b = total.T.astype(BF16)
        high, low = split((sums + gc_in[...]).T[:K])
        outs[0][...] = grad_b
        for peer in range(XL * Z * CORE):
            outs[1][peer] = jnp.concatenate([high, low], axis=0)


def local(place, target, pieces, b_full, *before):
    last = bool(before)
    steps, shift = (3, 1) if last else (1, 0)

    def tile(q):
        dc, dx = q // 2, q % 2

        def index(s, place):
            p = place[0]
            z = (lax.shift_right_logical(p, 1) + s + shift) & 3
            return 0, ((p & 8) ^ (8 * dx)) + z * 2 + ((p & 1) ^ dc), 0, 0

        return pl.BlockSpec((K, 1, SHARD, NJ), index)

    def whole(*shape):
        return pl.BlockSpec(shape, lambda s, place: (0,) * len(shape))

    anywhere = pl.BlockSpec(memory_space=pl.ANY)
    out = pl.BlockSpec((1, SHARD, R), lambda s, place: (s + shift, 0, 0))
    if last:
        after, carried = [((NJ, R), BF16), ((XL * Z * CORE, 2 * K, R), BF16)], [whole(R, NJ), whole(R, 128)] + [anywhere] * 4
    else:
        after, carried = [((R, NJ), F32), ((R, 128), F32)], []
    return pl.pallas_call(
        functools.partial(body, last),
        grid_spec=pltpu.PrefetchScalarGridSpec(
            num_scalar_prefetch=1,
            grid=(steps,),
            in_specs=[tile(q) for q in range(4)] + [whole(steps, 2 * SHARD, R)] * 2 + [whole(PEERS, NB + K, R)] + carried,
            out_specs=[out] * 4 + [whole(*shape) for shape, _ in after],
            scratch_shapes=[
                pltpu.VMEM((K, R, NJ), F32),
                pltpu.VMEM((GROUP, R), BF16),
            ],
        ),
        out_shape=[jax.ShapeDtypeStruct((Z, SHARD, R), F32)] * 4
        + [jax.ShapeDtypeStruct(shape, dtype) for shape, dtype in after],
        input_output_aliases={10 + i: i for i in range(4)} if last else {},
        compiler_params=pltpu.CompilerParams(vmem_limit_bytes=VMEM_LIMIT),
        cost_estimate=pl.CostEstimate(
            flops=3_230_000_000 * steps, bytes_accessed=5_500_000 * steps, transcendentals=2_100_000 * steps
        ),
        name="rest" if last else "begin",
    )(place, target, target, target, target, *pieces, b_full, *before)


def total(ref, first, rows):
    out = ref[0, first : first + rows].astype(F32)
    for peer in range(1, ref.shape[0]):
        out = out + ref[peer, first : first + rows].astype(F32)
    return out


def small(body, name, *out_shape, room=8):
    shapes = [jax.ShapeDtypeStruct(shape, dtype) for shape, dtype in out_shape]
    return pl.pallas_call(body, out_shape=shapes, compiler_params=pltpu.CompilerParams(vmem_limit_bytes=room << 20), name=name)


def repeat(b_ref, c_ref, out_ref):
    c = c_ref[...]
    for peer in range(PEERS):
        out_ref[peer, :NB] = b_ref[...]
        out_ref[peer, NB:] = c


def stack(*refs):
    for i, ref in enumerate(refs[:-1]):
        refs[-1][i] = ref[...]


def join(x_ref, y_ref, out_ref):
    out_ref[...] = (x_ref[...] + y_ref[...]).astype(BF16)


def pack(times_ref, gb_ref, out_ref):
    high, low = split(total(times_ref, 0, K) + total(times_ref, K, K))
    tail = jnp.concatenate([high, low], axis=0)
    for peer in range(PEERS):
        out_ref[peer, :NB] = gb_ref[peer * NB : (peer + 1) * NB]
        out_ref[peer, NB:] = tail


def spread(x_ref, y_ref, across_ref, own_ref, *out_refs):
    own_ref[...] = x_ref[0] + y_ref[0] + across_ref[0].astype(F32)
    for d, ref in zip(AWAY, out_refs):
        ref[...] = (x_ref[d] + y_ref[d] + across_ref[d].astype(F32)).astype(BF16)


def finish(first_ref, own_ref, g1, g2, g3, grad_a, grad_b, grad_c):
    grad_a[...] = own_ref[...] + g1[...].astype(F32) + g2[...].astype(F32) + g3[...].astype(F32)
    grad_b[...] = total(first_ref, 0, NB)
    grad_c[...] = total(first_ref, NB, K) + total(first_ref, NB + K, K)


def on_device(target, a_factor, b_factor, c_factor):
    place = lax.axis_index("space").astype(jnp.int32).reshape(1)
    (b_wide,) = small(repeat, "repeat", ((PEERS, NB + K, R), BF16), room=60)(b_factor, c_factor)
    b_full = lax.all_to_all(b_wide, "samples", 0, 0)
    a_x = lax.ppermute(a_factor, "space", TO_XL)
    pair = jnp.concatenate([a_factor, a_x], axis=0)
    mine = [lax.ppermute(pair, "space", from_z(d)) if d else pair for d in range(Z)]
    target = target.reshape(K, 16, SHARD, NJ)
    *parts, gb, gc = local(place, target, [pair[None], lax.ppermute(pair, "space", TO_CORE)[None]], b_full)
    *mine, gc = lax.optimization_barrier((*mine[1:], gc))
    (mine,) = small(stack, "stack", ((Z - 1, 2 * SHARD, R), BF16))(*mine)
    pieces = [mine, lax.ppermute(mine, "space", TO_CORE)]
    own, far, own_core, far_core, first, times = local(place, target, pieces, b_full, gb, gc, *parts)

    far_core = lax.ppermute(far_core, "space", TO_CORE)
    own_core = lax.ppermute(own_core, "space", TO_CORE)
    times = lax.all_to_all(times, "space", 0, 0)
    times, far_core = lax.optimization_barrier((times, far_core))
    (across,) = small(join, "join", ((Z, SHARD, R), BF16))(far, far_core)
    across = lax.ppermute(across, "space", TO_XL)
    (first,) = small(pack, "pack", ((PEERS, NB + 2 * K, R), BF16))(times, first)
    first = lax.all_to_all(first, "samples", 0, 0)
    piece = (SHARD, R)
    own, *away = small(spread, "spread", (piece, F32), *[(piece, BF16)] * 3)(own, own_core, across)
    away = [lax.ppermute(x, "space", from_z(-d)) for d, x in zip(AWAY, away)]
    first, *away = lax.optimization_barrier((first, *away))
    return tuple(small(finish, "finish", (piece, F32), ((NB, R), F32), ((K, R), F32))(first, own, *away))


def solution(mesh):
    return jax.shard_map(
        on_device,
        mesh=mesh,
        in_specs=(
            P(None, "samples", "space"),
            P(("samples", "space"), None),
            P(("space", "samples"), None),
            P(),
        ),
        out_specs=(P(("samples", "space"), None), P(("space", "samples"), None), P()),
        check_vma=False,
    )
```

```python
import functools

import jax
import jax.numpy as jnp
from jax import lax
from jax.experimental import pallas as pl
from jax.experimental.pallas import tpu as pltpu
from jax.sharding import PartitionSpec as P

F32 = jnp.float32
BF16 = jnp.bfloat16
K, R = 8, 256
SHARD = 128
NB, NJ = 64, 512
XL, Z, CORE = 2, 4, 2
PEERS = 8
AWAY = 2, 1, 3

SPACE = range(XL * Z * CORE)
TO_CORE = [(p, p ^ 1) for p in SPACE]
TO_XL = [(p, p ^ 8) for p in SPACE]


def from_z(d):
    return [((p & 9) | ((((p >> 1) + d) % 4) << 1), p) for p in SPACE]


def dot_last(x, y):
    return lax.dot_general(x, y, (((1,), (1,)), ((), ())), preferred_element_type=F32)


def dot(x, y):
    return jnp.dot(x, y, preferred_element_type=F32)


def split(x):
    high = x.astype(BF16)
    return high, (x - high.astype(F32)).astype(BF16)


GROUP = 4 * SHARD
VMEM_LIMIT = 44 << 20


def body(last, place, t0, t1, t2, t3, *refs):
    steps = 3 if last else 1
    mine, theirs, refs = refs[0], refs[1], refs[2:]
    b_ref, c_ref, refs = refs[0], refs[1], refs[2:]
    if last:
        gb_in, gc_in, refs = refs[0], refs[1], refs[6:]
    parts, outs, w_ref, a_ref = refs[:4], refs[4:-2], refs[-2], refs[-1]
    step = pl.program_id(0)
    a_ref[: 2 * SHARD] = mine[step]
    a_ref[2 * SHARD :] = theirs[step]
    rows = a_ref[...]
    wide = rows.astype(F32)
    rows_t = rows.T
    b = b_ref[...]
    c_half = c_ref[...]
    grad = jnp.zeros((GROUP, R), F32)
    def model(k):
        return dot_last((wide * c_half[k : k + 1, :]).astype(BF16), b)

    half = model(0)
    for k in range(K):
        t = (jnp.concatenate([r[k, 0] for r in (t0, t1, t2, t3)], axis=0)).astype(F32)
        d2 = ((jnp.tanh(half) + 1.0) - (t + t)).astype(BF16)
        if k + 1 < K:
            half = model(k + 1)
        part = dot(rows_t, d2)
        w_ref[k] = jnp.where(step > 0, w_ref[k], 0.0) + part if last else part
        grad = grad + dot(d2, b) * c_half[k : k + 1, :]

    for slot in range(4):
        parts[slot][0] = grad[slot * SHARD : (slot + 1) * SHARD]

    @pl.when(step == steps - 1)
    def _():
        total = gb_in[...] if last else jnp.zeros((R, NJ), F32)
        lane = lax.broadcasted_iota(jnp.int32, (R, 128), 1)
        sums = jnp.zeros((R, 128), F32)
        bt = b_ref[...].T.astype(F32)
        c_t = jnp.concatenate([c_half, jnp.zeros((128 - K, R), F32)], axis=0).T
        for k in range(K):
            wk = w_ref[k]
            total = total + wk * c_t[:, k : k + 1]
            s = jnp.sum(wk * bt, axis=1, keepdims=True) * 0.5
            sums = jnp.where(lane == k, s, sums)
        if not last:
            outs[0][...] = total
            outs[1][...] = sums
            return
        grad_b = total.T.astype(BF16)
        high, low = split((sums + gc_in[...]).T[:K])
        outs[0][...] = grad_b
        for peer in range(XL * Z * CORE):
            outs[1][peer] = jnp.concatenate([high, low], axis=0)


def local(place, target, pieces, b_full, c_half, *before):
    last = bool(before)
    steps, shift = (3, 1) if last else (1, 0)

    def tile(q):
        dc, dx = q // 2, q % 2

        def index(s, place):
            p = place[0]
            z = (lax.shift_right_logical(p, 1) + s + shift) & 3
            return 0, ((p & 8) ^ (8 * dx)) + z * 2 + ((p & 1) ^ dc), 0, 0

        return pl.BlockSpec((K, 1, SHARD, NJ), index)

    def whole(*shape):
        return pl.BlockSpec(shape, lambda s, place: (0,) * len(shape))

    anywhere = pl.BlockSpec(memory_space=pl.ANY)
    out = pl.BlockSpec((1, SHARD, R), lambda s, place: (s + shift, 0, 0))
    if last:
        after, carried = [((NJ, R), BF16), ((XL * Z * CORE, 2 * K, R), BF16)], [whole(R, NJ), whole(R, 128)] + [anywhere] * 4
    else:
        after, carried = [((R, NJ), F32), ((R, 128), F32)], []
    return pl.pallas_call(
        functools.partial(body, last),
        grid_spec=pltpu.PrefetchScalarGridSpec(
            num_scalar_prefetch=1,
            grid=(steps,),
            in_specs=[tile(q) for q in range(4)] + [whole(steps, 2 * SHARD, R)] * 2 + [whole(NJ, R), whole(K, R)] + carried,
            out_specs=[out] * 4 + [whole(*shape) for shape, _ in after],
            scratch_shapes=[
                pltpu.VMEM((K, R, NJ), F32),
                pltpu.VMEM((GROUP, R), BF16),
            ],
        ),
        out_shape=[jax.ShapeDtypeStruct((Z, SHARD, R), F32)] * 4
        + [jax.ShapeDtypeStruct(shape, dtype) for shape, dtype in after],
        input_output_aliases={11 + i: i for i in range(4)} if last else {},
        compiler_params=pltpu.CompilerParams(vmem_limit_bytes=VMEM_LIMIT),
        cost_estimate=pl.CostEstimate(
            flops=3_230_000_000 * steps, bytes_accessed=5_500_000 * steps, transcendentals=2_100_000 * steps
        ),
        name="rest" if last else "begin",
    )(place, target, target, target, target, *pieces, b_full, c_half, *before)


def total(ref, first, rows):
    out = ref[0, first : first + rows].astype(F32)
    for peer in range(1, ref.shape[0]):
        out = out + ref[peer, first : first + rows].astype(F32)
    return out


def small(body, name, *out_shape, room=8):
    shapes = [jax.ShapeDtypeStruct(shape, dtype) for shape, dtype in out_shape]
    return pl.pallas_call(body, out_shape=shapes, compiler_params=pltpu.CompilerParams(vmem_limit_bytes=room << 20), name=name)


def repeat(x_ref, out_ref):
    for peer in range(PEERS):
        out_ref[peer] = x_ref[...]


def stack(*refs):
    for i, ref in enumerate(refs[:-1]):
        refs[-1][i] = ref[...]


def join(x_ref, y_ref, out_ref):
    out_ref[...] = (x_ref[...] + y_ref[...]).astype(BF16)


def pack(times_ref, gb_ref, out_ref):
    high, low = split(total(times_ref, 0, K) + total(times_ref, K, K))
    tail = jnp.concatenate([high, low], axis=0)
    for peer in range(PEERS):
        out_ref[peer, :NB] = gb_ref[peer * NB : (peer + 1) * NB]
        out_ref[peer, NB:] = tail


def spread(x_ref, y_ref, across_ref, own_ref, *out_refs):
    own_ref[...] = x_ref[0] + y_ref[0] + across_ref[0].astype(F32)
    for d, ref in zip(AWAY, out_refs):
        ref[...] = (x_ref[d] + y_ref[d] + across_ref[d].astype(F32)).astype(BF16)


def finish(first_ref, own_ref, g1, g2, g3, grad_a, grad_b, grad_c):
    grad_a[...] = own_ref[...] + g1[...].astype(F32) + g2[...].astype(F32) + g3[...].astype(F32)
    grad_b[...] = total(first_ref, 0, NB)
    grad_c[...] = total(first_ref, NB, K) + total(first_ref, NB + K, K)


def on_device(target, a_factor, b_factor, c_factor):
    place = lax.axis_index("space").astype(jnp.int32).reshape(1)
    (b_wide,) = small(repeat, "repeat", ((PEERS, NB, R), BF16), room=60)(b_factor)
    b_full = lax.all_to_all(b_wide, "samples", 0, 0).reshape(NJ, R)
    c_half = c_factor.astype(F32) * 0.5
    a_x = lax.ppermute(a_factor, "space", TO_XL)
    pair = jnp.concatenate([a_factor, a_x], axis=0)
    mine = [lax.ppermute(pair, "space", from_z(d)) if d else pair for d in range(Z)]
    target = target.reshape(K, 16, SHARD, NJ)
    *parts, gb, gc = local(place, target, [pair[None], lax.ppermute(pair, "space", TO_CORE)[None]], b_full, c_half)
    *mine, gc = lax.optimization_barrier((*mine[1:], gc))
    (mine,) = small(stack, "stack", ((Z - 1, 2 * SHARD, R), BF16))(*mine)
    pieces = [mine, lax.ppermute(mine, "space", TO_CORE)]
    own, far, own_core, far_core, first, times = local(place, target, pieces, b_full, c_half, gb, gc, *parts)

    far_core = lax.ppermute(far_core, "space", TO_CORE)
    own_core = lax.ppermute(own_core, "space", TO_CORE)
    times = lax.all_to_all(times, "space", 0, 0)
    times, far_core = lax.optimization_barrier((times, far_core))
    (across,) = small(join, "join", ((Z, SHARD, R), BF16))(far, far_core)
    across = lax.ppermute(across, "space", TO_XL)
    (first,) = small(pack, "pack", ((PEERS, NB + 2 * K, R), BF16))(times, first)
    first = lax.all_to_all(first, "samples", 0, 0)
    piece = (SHARD, R)
    own, *away = small(spread, "spread", (piece, F32), *[(piece, BF16)] * 3)(own, own_core, across)
    away = [lax.ppermute(x, "space", from_z(-d)) for d, x in zip(AWAY, away)]
    first, *away = lax.optimization_barrier((first, *away))
    return tuple(small(finish, "finish", (piece, F32), ((NB, R), F32), ((K, R), F32))(first, own, *away))


def solution(mesh):
    return jax.shard_map(
        on_device,
        mesh=mesh,
        in_specs=(
            P(None, "samples", "space"),
            P(("samples", "space"), None),
            P(("space", "samples"), None),
            P(),
        ),
        out_specs=(P(("samples", "space"), None), P(("space", "samples"), None), P()),
        check_vma=False,
    )
```
